32 devices in a mesh: head: 2 (over y), seq: 16 (over z, x, core).
Axes of the slice: x: 2, y: 2, z: 4, core: 2. Of those that a mesh axis runs over, the one named last changes fastest.
Arguments:
- latent_q: bfloat16 [32, 128, 576], P(None, 'head'), may hold values from -13 to 13
- latent_keys: bfloat16 [16384, 576], P('seq'), may hold values from -10 to 10
- idx_q: bfloat16 [32, 64, 128], replicated, may hold values from -1.5 to 1.5
- idx_keys: bfloat16 [16, 1024, 128], P('seq', 'head'), may hold values from -1.5 to 1.5
- idx_weight: bfloat16 [32, 64], replicated, may hold values from -1.8 to 1.8
Outputs:
- loss: float32 [], replicated
- query_grad: float32 [2048, 128], P(('head', 'seq'))
- weight_grad: float32 [2048], P(('head', 'seq'))
- key_grad: float32 [16, 1024, 128], P('seq', 'head')
The draws below stay inside these ranges and needn't reach their ends.
All inputs are finite; a program needn't handle non-finite values.
Results may differ from the reference program's by a relative error of at most 0.0027.
Values may be sent and summed in bfloat16 or wider, within the bound.
A program may use at most 64 MiB of HBM per device.

```python
import math
import jax
import jax.numpy as jnp
from jax import lax

H = 128
KV_RANK = 512
ROPE = 64
IDX_HEADS = 64
IDX_D = 128
Q = 32
KEY_DEV = 1024
KEYS = 16384
N_SEQ = 16


def draw_everything(key):
    streams = jax.random.split(jax.random.fold_in(key, 7), 6)
    count = KEY_DEV * N_SEQ
    width = KV_RANK + ROPE
    cache = jnp.clip(jax.random.normal(streams[0], (count, width), jnp.float32), -5.0, 5.0)
    row_scale = jnp.exp(jax.random.uniform(streams[1], (count, 1), jnp.float32, math.log(0.5), math.log(2.0)))
    cache = cache * row_scale
    queries = jnp.clip(jax.random.normal(streams[2], (Q, H, width), jnp.float32), -5.0, 5.0)
    index_keys = 0.3 * jnp.clip(jax.random.normal(streams[3], (count, IDX_D), jnp.float32), -5.0, 5.0)
    index_queries = 0.3 * jnp.clip(jax.random.normal(streams[4], (Q, IDX_HEADS, IDX_D), jnp.float32), -5.0, 5.0)
    head_weights = 0.6 * jnp.clip(jax.random.normal(streams[5], (Q, IDX_HEADS), jnp.float32), -3.0, 3.0)
    return (queries, cache, index_queries, index_keys.reshape(N_SEQ, KEY_DEV, IDX_D), head_weights)


def draw_latent_q(key, part):
    return draw_everything(key)[0].astype(jnp.bfloat16)


def draw_latent_keys(key, part):
    return draw_everything(key)[1].astype(jnp.bfloat16)


def draw_idx_q(key, part):
    return draw_everything(key)[2].astype(jnp.bfloat16)


def draw_idx_keys(key, part):
    return draw_everything(key)[3].astype(jnp.bfloat16)


def draw_idx_weight(key, part):
    return draw_everything(key)[4].astype(jnp.bfloat16)


def setup_inputs(seed: int = 0) -> dict:
    arg_keys = jax.random.split(jax.random.key(seed), 6)
    return {
        "latent_q": draw_latent_q(jax.random.fold_in(arg_keys[5], 71), 0),
        "latent_keys": draw_latent_keys(jax.random.fold_in(arg_keys[5], 71), 0),
        "idx_q": draw_idx_q(jax.random.fold_in(arg_keys[5], 71), 0),
        "idx_keys": draw_idx_keys(jax.random.fold_in(arg_keys[5], 71), 0),
        "idx_weight": draw_idx_weight(jax.random.fold_in(arg_keys[5], 71), 0),
    }


softmax_scale = 192 ** -0.5


def plogp(values):
    safe = jnp.where(values > 0, values, 1.0)
    return jnp.where(values > 0, values * jnp.log(safe), 0.0)


def reference(latent_q, latent_keys, idx_q, idx_keys, idx_weight):
    def attend(acc, head_q):
        scores = jnp.dot(head_q, latent_keys.T, preferred_element_type=jnp.float32) * softmax_scale
        top = jnp.max(scores, axis=1, keepdims=True)
        expo = jnp.exp(scores - top)
        return acc + expo / jnp.sum(expo, axis=1, keepdims=True), None

    summed, _ = lax.scan(attend, jnp.zeros((Q, KEYS), jnp.float32), jnp.swapaxes(latent_q, 0, 1))
    targets = summed / H
    keys_flat = idx_keys.reshape(KEYS, IDX_D)
    weights = idx_weight.astype(jnp.float32)
    head_queries = jnp.swapaxes(idx_q, 0, 1)
    head_weights = weights.T

    def score_head(acc, pair):
        head_q, head_w = pair
        act = jnp.dot(head_q, keys_flat.T, preferred_element_type=jnp.float32)
        return acc + head_w[:, None] * jnp.maximum(act, 0.0), None

    logits, _ = lax.scan(score_head, jnp.zeros((Q, KEYS), jnp.float32), (head_queries, head_weights))
    top = jnp.max(logits, axis=1, keepdims=True)
    expo = jnp.exp(logits - top)
    total = jnp.sum(expo, axis=1, keepdims=True)
    loss = jnp.sum(plogp(targets) - targets * (logits - top - jnp.log(total))) / Q
    grad = expo / total - targets

    def back_head(dkeys, pair):
        head_q, head_w = pair
        act = jnp.dot(head_q, keys_flat.T, preferred_element_type=jnp.float32)
        dweight = jnp.sum(grad * jnp.maximum(act, 0.0), axis=1)
        dact = jnp.where(act > 0, grad * head_w[:, None], 0.0).astype(jnp.bfloat16)
        dquery = jnp.dot(dact, keys_flat, preferred_element_type=jnp.float32)
        dkeys = dkeys + jnp.dot(dact.T, head_q, preferred_element_type=jnp.float32)
        return dkeys, (dquery, dweight)

    dkeys, (dquery, dweight) = lax.scan(back_head, jnp.zeros((KEYS, IDX_D), jnp.float32), (head_queries, head_weights))
    return (loss, dquery.reshape(IDX_HEADS * Q, IDX_D), dweight.reshape(IDX_HEADS * Q),
            dkeys.reshape(N_SEQ, KEY_DEV, IDX_D))
```

```python
import functools
import math

import jax
import jax.numpy as jnp
from jax import lax
from jax.experimental import pallas as pl
from jax.experimental.pallas import tpu as pltpu
from jax.sharding import PartitionSpec as P

MESH = pl.DeviceIdType.MESH
NT = (((1,), (1,)), ((), ()))
TN = (((0,), (0,)), ((), ()))
F32 = jnp.float32
BF16 = jnp.bfloat16

exponent_scale = 192 ** (-0.5) * math.log2(math.e)


def to_row(column):
    wide = jnp.broadcast_to(column, (column.shape[0], 128))
    copies = 128 // column.shape[0]
    return jnp.concatenate([wide] * copies, axis=0).T[0:1, :]


def to_column(row, count):
    return jnp.broadcast_to(row, (128, 128)).T[0:count, 0:1]


def join_log2(values):
    top = jnp.max(values, axis=0)
    return top + jnp.log2(jnp.sum(jnp.exp2(values - top[None]), axis=0))


def join_log(values):
    top = jnp.max(values, axis=0)
    return top + jnp.log(jnp.sum(jnp.exp(values - top[None]), axis=0))


def kernel(
    heads_axis, seq_axis, heads, queries_count,
    latent_q_hbm, turned_keys_hbm, query_hbm, keys_hbm, weight_hbm,
    loss_out, query_out, prod_out, key_out,
    latent_q, turned_keys, query_ref, keys_ref, weight_ref, load_sem,
    latent_keys, scores_a, scores_b, top_a, top_b,
    idx_q, flat_queries, weights, own_term, pair_recv, index_all, expo, base, spread, stat_all, sum_send, sum_recv, act, dact, term_a, recv_a, term_b, recv_b, loss_all,
    stat_send_sem, stat_recv_sem, sum_send_sem, sum_recv_sem,
    a_send_sem, a_recv_sem, b_send_sem, b_recv_sem, loss_send_sem, loss_recv_sem, pair_send_sem, pair_recv_sem, index_send_sem, index_recv_sem,
):
    my_head = lax.axis_index("head")
    my_seq = lax.axis_index("seq")
    devices = heads_axis * seq_axis
    me = my_head * seq_axis + my_seq
    barrier = pltpu.get_barrier_semaphore()
    rows, width = latent_q.shape
    local_heads = rows // queries_count
    halves, _, half_rows = expo.shape
    half_queries = queries_count // halves
    tile = top_a.shape[1]
    tiles = rows // tile

    def place(index):
        return (index // seq_axis, lax.rem(index, seq_axis))

    loads = [pltpu.make_async_copy(turned_keys_hbm, turned_keys, load_sem.at[0])]
    for j in range(halves):
        part = pl.ds(j * half_rows, half_rows)
        loads.append(pltpu.make_async_copy(latent_q_hbm.at[part], latent_q.at[part], load_sem.at[1 + j]))
    loads.append(pltpu.make_async_copy(query_hbm, query_ref, load_sem.at[halves + 1]))
    loads.append(pltpu.make_async_copy(keys_hbm, keys_ref, load_sem.at[halves + 2]))
    loads.append(pltpu.make_async_copy(weight_hbm, weight_ref, load_sem.at[halves + 3]))
    for load in loads:
        load.start()

    def greet(offset, carry):
        other = lax.rem(me + offset, devices)
        pl.semaphore_signal(barrier, inc=1, device_id=place(other), device_id_type=MESH)
        return carry

    lax.fori_loop(1, devices, greet, 0)

    def stat_copy(half, offset, source, target):
        return pltpu.make_async_remote_copy(
            src_ref=stat_all.at[source, half],
            dst_ref=stat_all.at[source, half],
            send_sem=stat_send_sem.at[offset, half],
            recv_sem=stat_recv_sem.at[source, half],
            device_id=(my_head, target),
            device_id_type=MESH,
        )

    def stat_start(half):
        def start(offset, carry):
            stat_copy(half, offset, my_seq, lax.rem(my_seq + offset, seq_axis)).start()
            return carry

        lax.fori_loop(1, seq_axis, start, 0)

    def stat_wait(half):
        def wait(offset, carry):
            other = lax.rem(my_seq + offset, seq_axis)
            stat_copy(half, offset, other, other).wait_recv()
            return carry

        lax.fori_loop(1, seq_axis, wait, 0)

    def stat_sent(half):
        def sent(offset, carry):
            stat_copy(half, offset, my_seq, lax.rem(my_seq + offset, seq_axis)).wait_send()
            return carry

        lax.fori_loop(1, seq_axis, sent, 0)

    loads[0].wait()
    latent_keys[...] = turned_keys[...].T
    loads[1].wait()
    buffers = [(scores_a, top_a), (scores_b, top_b)]

    def multiply(t):
        buffer, top = buffers[t % 2]
        scores = lax.dot_general(
            latent_keys[...], latent_q[pl.ds(t * tile, tile), :], NT, preferred_element_type=F32
        )
        buffer[...] = scores
        top[...] = jnp.max(scores, axis=0, keepdims=True)

    def soften(t):
        buffer, top_ref = buffers[t % 2]
        top = top_ref[...]
        part = jnp.exp2((buffer[...] - top) * exponent_scale)
        half = t * tile // half_rows
        start = t * tile - half * half_rows
        expo[half, :, start : start + tile] = part.astype(BF16)
        total = jnp.sum(part, axis=0, keepdims=True)
        scaled = top * exponent_scale
        joint = scaled + jnp.log2(total)
        for j in range(tile // 128):
            row = start // 128 + j
            base[half, row : row + 1, :] = scaled[:, j * 128 : (j + 1) * 128]
            stat_all[my_seq, half, row : row + 1, :] = joint[:, j * 128 : (j + 1) * 128]

    early = (tiles * 3) // 4
    for t in range(tiles):
        if t * tile == half_rows:
            for j in range(2, halves + 1):
                loads[j].wait()
        multiply(t)
        if t:
            soften(t - 1)
        if t == early:
            pl.semaphore_wait(barrier, devices - 1)
            stat_start(0)
    soften(tiles - 1)
    stat_start(1)

    def index_copy(offset, source, target):
        return pltpu.make_async_remote_copy(
            src_ref=index_all.at[source],
            dst_ref=index_all.at[source],
            send_sem=index_send_sem.at[offset],
            recv_sem=index_recv_sem.at[source],
            device_id=place(target),
            device_id_type=MESH,
        )

    def index_start(offset, carry):
        index_copy(offset, me, lax.rem(me + offset, devices)).start()
        return carry

    def index_wait(offset, carry):
        other = lax.rem(me + offset, devices)
        index_copy(offset, other, other).wait_recv()
        return carry

    def index_sent(offset, carry):
        index_copy(offset, me, lax.rem(me + offset, devices)).wait_send()
        return carry

    for j in range(3):
        loads[halves + 1 + j].wait()
    blocks, block, _ = weights.shape
    fine = keys_ref.shape[0]
    group = math.gcd(blocks, 8)
    heads_in_block = block // queries_count
    wide = weight_ref[...].astype(F32)
    flat_queries[...] = query_ref[...].astype(F32)
    index_heads = wide.shape[1]
    for g in range(wide.shape[1]):
        row = g % heads_in_block * queries_count
        weights[g // heads_in_block, row : row + queries_count, :] = wide[:, g : g + 1]
        picked = flat_queries[pl.ds(g, queries_count, stride=index_heads), :]
        idx_q[g // heads_in_block, row : row + queries_count, :] = picked.astype(BF16)

    def index_scores(i, logits):
        queries = idx_q[pl.ds(i * group, group)]
        part = lax.dot_general(
            queries.reshape(group * block, -1), keys_ref[...], NT, preferred_element_type=F32
        )
        part = part.reshape(group, block, fine)
        act[pl.ds(i * group, group)] = part
        weighted = weights[pl.ds(i * group, group)] * jnp.maximum(part, 0.0)
        return logits + jnp.sum(
            weighted.reshape(group * heads_in_block, queries_count, fine), axis=0
        )

    logits = lax.fori_loop(
        0, blocks // group, index_scores, jnp.zeros((queries_count, fine), F32)
    )
    index_top = jnp.max(logits, axis=1, keepdims=True)
    index_total = jnp.sum(jnp.exp(logits - index_top), axis=1, keepdims=True)
    index_all[me] = to_row(index_top + jnp.log(index_total))
    lax.fori_loop(1, devices, index_start, 0)

    def sum_copy(half, offset, block_index, slot, target):
        return pltpu.make_async_remote_copy(
            src_ref=sum_send.at[block_index, half],
            dst_ref=sum_recv.at[slot, half],
            send_sem=sum_send_sem.at[offset, half],
            recv_sem=sum_recv_sem.at[slot, half],
            device_id=(target, my_seq),
            device_id_type=MESH,
        )

    def combine(half, target):
        mine = expo[half, pl.ds(pl.multiple_of(target * fine, fine), fine), :]
        both = lax.dot_general(spread[half], mine, NT, preferred_element_type=F32)
        return both[0:half_queries] + both[half_queries : 2 * half_queries]

    own_parts = []
    for half in range(halves):
        stat_wait(half)
        factor = jnp.exp2(base[half] - join_log2(stat_all[:, half]))
        upper = factor.astype(BF16).astype(F32)
        lower = factor - upper
        first = lax.broadcasted_iota(jnp.int32, (half_queries, 128), 0) * local_heads
        for j in range(half_rows // 128):
            lane = lax.broadcasted_iota(jnp.int32, (half_queries, 128), 1) + j * 128
            inside = jnp.logical_and(lane >= first, lane < first + local_heads)
            columns = slice(j * 128, (j + 1) * 128)
            spread[half, 0:half_queries, columns] = jnp.where(
                inside, upper[j : j + 1, :], 0.0
            ).astype(BF16)
            spread[half, half_queries : 2 * half_queries, columns] = jnp.where(
                inside, lower[j : j + 1, :], 0.0
            ).astype(BF16)
        for offset in range(1, heads_axis):
            target = lax.rem(my_head + offset, heads_axis)
            sum_send[target, half] = combine(half, target)
            sum_copy(half, offset, target, my_head, target).start()
        own_parts.append(combine(half, my_head))

    for half in range(halves):
        for offset in range(1, heads_axis):
            source = lax.rem(my_head + offset, heads_axis)
            sum_copy(half, offset, source, source, source).wait_recv()
            own_parts[half] = own_parts[half] + sum_recv[source, half]
    targets = jnp.concatenate(own_parts, axis=0) / heads
    lax.fori_loop(1, devices, index_wait, 0)
    index_log = to_column(join_log(index_all[...]), queries_count)
    shifted = logits - index_log
    positive = targets > 0
    own_loss = jnp.where(positive, targets * jnp.log(jnp.where(positive, targets, 1.0)), 0.0)
    own_loss = jnp.sum(own_loss - targets * shifted, axis=0, keepdims=True)
    own_loss = sum(own_loss[:, i * 128 : (i + 1) * 128] for i in range(fine // 128))
    grad = jnp.exp(shifted) - targets
    loss_all[me] = own_loss

    def loss_copy(offset, slot, target):
        return pltpu.make_async_remote_copy(
            src_ref=loss_all.at[slot],
            dst_ref=loss_all.at[slot],
            send_sem=loss_send_sem.at[offset],
            recv_sem=loss_recv_sem.at[slot],
            device_id=place(target),
            device_id_type=MESH,
        )

    chunk = own_term.shape[1]
    owners = block // chunk
    depth, peers = term_a.shape[0:2]
    inner = seq_axis // depth
    lanes = inner // 2
    my_depth = my_seq // inner
    my_inner = lax.rem(my_seq, inner)
    parity = lax.rem(my_seq, 2)
    pair = my_seq + 1 - 2 * parity
    my_peer = my_head * lanes + my_inner // 2

    def peer_at(offset):
        return lax.rem(my_peer + offset, peers)

    def depth_at(distance):
        return lax.rem(my_depth + distance, depth)

    def owner_of(layer, peer, side):
        return (peer // lanes) * seq_axis + layer * inner + 2 * lax.rem(peer, lanes) + side

    def pair_copy(layer, peer, side):
        owner = owner_of(layer, peer, side)
        return pltpu.make_async_remote_copy(
            src_ref=own_term.at[owner],
            dst_ref=pair_recv.at[owner],
            send_sem=pair_send_sem.at[layer, peer],
            recv_sem=pair_recv_sem.at[layer, peer],
            device_id=(my_head, pair),
            device_id_type=MESH,
        )

    def plane_copy(layer, source_slot, slot, target):
        return pltpu.make_async_remote_copy(
            src_ref=term_a.at[layer, source_slot],
            dst_ref=recv_a.at[layer, slot],
            send_sem=a_send_sem.at[layer, source_slot],
            recv_sem=a_recv_sem.at[layer, slot],
            device_id=(target // lanes, my_depth * inner + 2 * lax.rem(target, lanes) + parity),
            device_id_type=MESH,
        )

    def depth_copy(source_slot, slot, target):
        return pltpu.make_async_remote_copy(
            src_ref=term_b.at[source_slot],
            dst_ref=recv_b.at[slot],
            send_sem=b_send_sem.at[source_slot],
            recv_sem=b_recv_sem.at[slot],
            device_id=(my_head, target * inner + my_inner),
            device_id_type=MESH,
        )

    grads = jnp.concatenate([grad] * heads_in_block, axis=0)
    grad_upper = grads.astype(BF16).astype(F32)
    grad_lower = grads - grad_upper

    def back(chosen):
        upper_parts, lower_parts = [], []
        for b in chosen:
            part = act[b]
            on = part > 0
            dact[b] = jnp.where(on, grads * weights[b], 0.0).astype(BF16)
            upper_parts.append(jnp.where(on, grad_upper, 0.0).astype(BF16))
            lower_parts.append(jnp.where(on, grad_lower, 0.0).astype(BF16))
        both = jnp.concatenate(upper_parts + lower_parts, axis=0)
        result = jnp.dot(both, keys_ref[...], preferred_element_type=F32)
        result = result[0 : block * len(chosen)] + result[block * len(chosen) :]
        for i, b in enumerate(chosen):
            for j in range(owners):
                start = i * block + j * chunk
                own_term[b * owners + j] = result[start : start + chunk]

    def pair_start(distance):
        for offset in range(peers):
            pair_copy(depth_at(distance), peer_at(offset), 1 - parity).start()

    def plane_start(distance):
        layer = depth_at(distance)
        for offset in range(1, peers):
            peer = peer_at(offset)
            owner = owner_of(layer, peer, parity)
            pair_copy(layer, peer, parity).wait_recv()
            term_a[layer, peer] = (own_term[owner] + pair_recv[owner]).astype(BF16)
            plane_copy(layer, peer, my_peer, peer).start()
        pair_copy(layer, my_peer, parity).wait_recv()

    def layer_order(step):
        return lax.rem(step + 1, depth)

    if owners == 1:

        def first_half(step, carry):
            distance = layer_order(step)
            layer = depth_at(distance)
            back([owner_of(layer, peer_at(offset), 1 - parity) for offset in range(peers)])
            pair_start(distance)
            return carry

        def second_half(step, carry):
            distance = layer_order(step)
            layer = depth_at(distance)
            back([owner_of(layer, peer_at(offset), parity) for offset in range(peers)])
            plane_start(distance)
            return carry

    else:

        def every_block(b, carry):
            back([b])
            return carry

        def first_half(step, carry):
            pair_start(layer_order(step))
            return carry

        def second_half(step, carry):
            plane_start(layer_order(step))
            return carry

        lax.fori_loop(0, blocks, every_block, 0)

    lax.fori_loop(0, depth, first_half, 0)
    lax.fori_loop(0, depth, second_half, 0)

    def loss_start(offset, carry):
        loss_copy(offset, me, lax.rem(me + offset, devices)).start()
        return carry

    lax.fori_loop(1, devices, loss_start, 0)

    key_out[...] = lax.dot_general(
        dact[...].reshape(blocks * block, fine),
        idx_q[...].reshape(blocks * block, -1),
        TN,
        preferred_element_type=F32,
    )

    for half in range(halves):
        stat_sent(half)
        for offset in range(1, heads_axis):
            target = lax.rem(my_head + offset, heads_axis)
            sum_copy(half, offset, target, my_head, target).wait_send()
    lax.fori_loop(1, devices, index_sent, 0)

    def pair_sent(step, carry):
        for offset in range(peers):
            pair_copy(step, peer_at(offset), 1 - parity).wait_send()
        return carry

    lax.fori_loop(0, depth, pair_sent, 0)

    def plane_total(layer):
        owner = owner_of(layer, my_peer, parity)
        total = own_term[owner] + pair_recv[owner]
        for offset in range(1, peers):
            source = peer_at(offset)
            plane_copy(layer, source, source, source).wait_recv()
            total = total + recv_a[layer, source].astype(F32)
        return total

    def depth_start(distance, carry):
        layer = depth_at(distance)
        term_b[layer] = plane_total(layer).astype(BF16)
        depth_copy(layer, my_depth, layer).start()
        return carry

    lax.fori_loop(1, depth, depth_start, 0)

    def depth_wait(distance, total):
        source = depth_at(distance)
        depth_copy(source, source, source).wait_recv()
        return total + recv_b[source].astype(F32)

    total = lax.fori_loop(1, depth, depth_wait, plane_total(my_depth))
    own_block = me // owners
    inside_block = me - own_block * owners
    own_weights = weights[own_block]
    own_queries = idx_q[own_block].astype(F32)
    if owners == 1:
        query_out[...] = total * own_weights
        prod_out[...] = total * own_queries
    else:
        for j in range(owners):

            @pl.when(inside_block == j)
            def _():
                query_out[...] = total * own_weights[j * chunk : (j + 1) * chunk]
                prod_out[...] = total * own_queries[j * chunk : (j + 1) * chunk]

    def loss_wait(offset, carry):
        source = lax.rem(me + offset, devices)
        loss_copy(offset, source, source).wait_recv()
        return carry

    lax.fori_loop(1, devices, loss_wait, 0)
    loss_out[...] = jnp.sum(loss_all[...], axis=0)

    def last_sent(offset, carry):
        other = lax.rem(me + offset, devices)
        loss_copy(offset, me, other).wait_send()
        return carry

    def plane_sent(layer, carry):
        for offset in range(1, peers):
            plane_copy(layer, peer_at(offset), my_peer, peer_at(offset)).wait_send()
        return carry

    def depth_sent(distance, carry):
        layer = depth_at(distance)
        depth_copy(layer, my_depth, layer).wait_send()
        return carry

    lax.fori_loop(1, devices, last_sent, 0)
    lax.fori_loop(0, depth, plane_sent, 0)
    lax.fori_loop(1, depth, depth_sent, 0)


def closing(queries_count, loss_in, query_in, prod_in, key_in, loss_out, query_out, weight_out, key_out):
    loss_out[...] = jnp.sum(loss_in[...], axis=1, keepdims=True) / queries_count
    query_out[...] = query_in[...]
    ones = jnp.ones((8, prod_in.shape[1]), F32)
    sums = lax.dot_general(
        ones, prod_in[...], NT, precision=lax.Precision.HIGHEST, preferred_element_type=F32
    )
    weight_out[...] = sums[0:1]
    key_out[...] = key_in[...]


def shards(heads_axis, seq_axis, latent_q, latent_keys, idx_q, idx_keys, idx_weight):
    queries_count, local_heads, width = latent_q.shape
    index_heads, size = idx_q.shape[1:]
    rows = queries_count * local_heads
    keys = latent_keys.shape[0]
    fine = idx_keys.shape[1]
    devices = heads_axis * seq_axis
    all_rows = queries_count * index_heads
    chunk = all_rows // devices
    block = max(chunk, queries_count)
    blocks = all_rows // block
    halves = 2
    half_rows = rows // halves
    half_queries = queries_count // halves
    tile = min(256, half_rows)
    inner = math.gcd(seq_axis, 4)
    depth = seq_axis // inner
    peers = heads_axis * inner // 2
    queries = idx_q.reshape(all_rows, size)
    vmem = pl.BlockSpec(memory_space=pltpu.VMEM)
    dma = pltpu.SemaphoreType.DMA
    loss, query_grad, prod, key_grad = pl.pallas_call(
        functools.partial(
            kernel, heads_axis, seq_axis, local_heads * heads_axis, queries_count
        ),
        out_shape=(
            jax.ShapeDtypeStruct((1, 128), F32),
            jax.ShapeDtypeStruct((chunk, size), F32),
            jax.ShapeDtypeStruct((chunk, size), F32),
            jax.ShapeDtypeStruct((fine, size), F32),
        ),
        in_specs=[pl.BlockSpec(memory_space=pl.ANY)] * 5,
        out_specs=(vmem,) * 4,
        scratch_shapes=[
            pltpu.VMEM((rows, width), BF16),
            pltpu.VMEM((width, keys), BF16),
            pltpu.VMEM((all_rows, size), BF16),
            pltpu.VMEM((fine, size), BF16),
            pltpu.VMEM((queries_count, index_heads), BF16),
            dma((halves + 4,)),
            pltpu.VMEM((keys, width), BF16),
            pltpu.VMEM((keys, tile), F32),
            pltpu.VMEM((keys, tile), F32),
            pltpu.VMEM((1, tile), F32),
            pltpu.VMEM((1, tile), F32),
            pltpu.VMEM((blocks, block, size), BF16),
            pltpu.VMEM((all_rows, size), F32),
            pltpu.VMEM((blocks, block, 1), F32),
            pltpu.VMEM((devices, chunk, size), F32),
            pltpu.VMEM((devices, chunk, size), F32),
            pltpu.VMEM((devices, 1, 128), F32),
            pltpu.VMEM((halves, keys, half_rows), BF16),
            pltpu.VMEM((halves, half_rows // 128, 128), F32),
            pltpu.VMEM((halves, 2 * half_queries, half_rows), BF16),
            pltpu.VMEM((seq_axis, halves, half_rows // 128, 128), F32),
            pltpu.VMEM((heads_axis, halves, half_queries, fine), F32),
            pltpu.VMEM((heads_axis, halves, half_queries, fine), F32),
            pltpu.VMEM((blocks, block, fine), F32),
            pltpu.VMEM((blocks, block, fine), BF16),
            pltpu.VMEM((depth, peers, chunk, size), BF16),
            pltpu.VMEM((depth, peers, chunk, size), BF16),
            pltpu.VMEM((depth, chunk, size), BF16),
            pltpu.VMEM((depth, chunk, size), BF16),
            pltpu.VMEM((devices, 1, 128), F32),
            dma((seq_axis, halves)),
            dma((seq_axis, halves)),
            dma((heads_axis, halves)),
            dma((heads_axis, halves)),
            dma((depth, peers)),
            dma((depth, peers)),
            dma((depth,)),
            dma((depth,)),
            dma((devices,)),
            dma((devices,)),
            dma((depth, peers)),
            dma((depth, peers)),
            dma((devices,)),
            dma((devices,)),
        ],
        compiler_params=pltpu.CompilerParams(
            collective_id=0, has_side_effects=True, vmem_limit_bytes=60 * 1024 * 1024
        ),
    )(latent_q.reshape(rows, width), latent_keys.T, queries, idx_keys[0], idx_weight)
    loss, query_grad, weight_grad, key_grad = pl.pallas_call(
        functools.partial(closing, queries_count),
        out_shape=(
            jax.ShapeDtypeStruct((1, 1), F32),
            jax.ShapeDtypeStruct((chunk, size), F32),
            jax.ShapeDtypeStruct((1, chunk), F32),
            jax.ShapeDtypeStruct((fine, size), F32),
        ),
        in_specs=[vmem] * 4,
        out_specs=(vmem,) * 4,
    )(loss, query_grad, prod, key_grad)
    return (loss.reshape(()), query_grad, weight_grad.reshape(-1), key_grad[None])


def solution(mesh):
    in_specs = (P(None, "head", None), P("seq", None), P(), P("seq", "head", None), P())
    out_specs = (P(), P(("head", "seq"), None), P(("head", "seq")), P("seq", "head", None))
    body = functools.partial(shards, mesh.shape["head"], mesh.shape["seq"])
    return jax.shard_map(body, mesh=mesh, in_specs=in_specs, out_specs=out_specs, check_vma=False)
```

```python
import functools
import math

import jax
import jax.numpy as jnp
from jax import lax
from jax.experimental import pallas as pl
from jax.experimental.pallas import tpu as pltpu
from jax.sharding import PartitionSpec as P

MESH = pl.DeviceIdType.MESH
NT = (((1,), (1,)), ((), ()))
TN = (((0,), (0,)), ((), ()))
F32 = jnp.float32
BF16 = jnp.bfloat16

exponent_scale = 192 ** (-0.5) * math.log2(math.e)


def to_row(column):
    wide = jnp.broadcast_to(column, (column.shape[0], 128))
    copies = 128 // column.shape[0]
    return jnp.concatenate([wide] * copies, axis=0).T[0:1, :]


def to_column(row, count):
    return jnp.broadcast_to(row, (128, 128)).T[0:count, 0:1]


def join_log2(values):
    top = jnp.max(values, axis=0)
    return top + jnp.log2(jnp.sum(jnp.exp2(values - top[None]), axis=0))


def join_log(values):
    top = jnp.max(values, axis=0)
    return top + jnp.log(jnp.sum(jnp.exp(values - top[None]), axis=0))


def kernel(
    heads_axis, seq_axis, heads, queries_count,
    latent_q_hbm, turned_keys_hbm, query_hbm, keys_hbm, weight_hbm,
    loss_out, query_out, prod_out, key_out,
    latent_q, turned_keys, query_ref, keys_ref, weight_ref, load_sem,
    latent_keys, scores_a, scores_b, top_a, top_b,
    idx_q, flat_queries, weights, own_term, pair_recv, index_all, expo, base, spread, stat_all, sum_send, sum_recv, act, dact, term_a, recv_a, term_b, recv_b, loss_all,
    stat_send_sem, stat_recv_sem, sum_send_sem, sum_recv_sem,
    a_send_sem, a_recv_sem, b_send_sem, b_recv_sem, loss_send_sem, loss_recv_sem, pair_send_sem, pair_recv_sem, index_send_sem, index_recv_sem,
):
    my_head = lax.axis_index("head")
    my_seq = lax.axis_index("seq")
    devices = heads_axis * seq_axis
    me = my_head * seq_axis + my_seq
    barrier = pltpu.get_barrier_semaphore()
    rows, width = latent_q.shape
    local_heads = rows // queries_count
    halves, _, half_rows = expo.shape
    half_queries = queries_count // halves
    tile = top_a.shape[1]
    tiles = rows // tile

    def place(index):
        return (index // seq_axis, lax.rem(index, seq_axis))

    loads = [pltpu.make_async_copy(turned_keys_hbm, turned_keys, load_sem.at[0])]
    for j in range(halves):
        part = pl.ds(j * half_rows, half_rows)
        loads.append(pltpu.make_async_copy(latent_q_hbm.at[part], latent_q.at[part], load_sem.at[1 + j]))
    loads.append(pltpu.make_async_copy(query_hbm, query_ref, load_sem.at[halves + 1]))
    loads.append(pltpu.make_async_copy(keys_hbm, keys_ref, load_sem.at[halves + 2]))
    loads.append(pltpu.make_async_copy(weight_hbm, weight_ref, load_sem.at[halves + 3]))
    for load in loads:
        load.start()

    def greet(offset, carry):
        other = lax.rem(me + offset, devices)
        pl.semaphore_signal(barrier, inc=1, device_id=place(other), device_id_type=MESH)
        return carry

    lax.fori_loop(1, devices, greet, 0)

    def stat_copy(half, slots, target):
        return pltpu.make_async_remote_copy(
            src_ref=stat_all.at[half, slots],
            dst_ref=stat_all.at[half, slots],
            send_sem=stat_send_sem.at[half],
            recv_sem=stat_recv_sem.at[half],
            device_id=(my_head, target),
            device_id_type=MESH,
        )

    def stat_start(half):
        def start(offset, carry):
            stat_copy(half, my_seq, lax.rem(my_seq + offset, seq_axis)).start()
            return carry

        lax.fori_loop(1, seq_axis, start, 0)

    other_seqs = pl.ds(0, seq_axis - 1)
    other_devices = pl.ds(0, devices - 1)

    loads[0].wait()
    latent_keys[...] = turned_keys[...].T
    loads[1].wait()
    buffers = [(scores_a, top_a), (scores_b, top_b)]

    def multiply(t):
        buffer, top = buffers[t % 2]
        scores = lax.dot_general(
            latent_keys[...], latent_q[pl.ds(t * tile, tile), :], NT, preferred_element_type=F32
        )
        buffer[...] = scores
        top[...] = jnp.max(scores, axis=0, keepdims=True)

    def soften(t):
        buffer, top_ref = buffers[t % 2]
        top = top_ref[...]
        part = jnp.exp2((buffer[...] - top) * exponent_scale)
        half = t * tile // half_rows
        start = t * tile - half * half_rows
        expo[half, :, start : start + tile] = part.astype(BF16)
        total = jnp.sum(part, axis=0, keepdims=True)
        scaled = top * exponent_scale
        joint = scaled + jnp.log2(total)
        for j in range(tile // 128):
            row = start // 128 + j
            base[half, row : row + 1, :] = scaled[:, j * 128 : (j + 1) * 128]
            stat_all[half, my_seq, row : row + 1, :] = joint[:, j * 128 : (j + 1) * 128]

    blocks, block, _ = weights.shape
    fine = keys_ref.shape[0]
    group = math.gcd(blocks, 8)
    heads_in_block = block // queries_count
    index_heads = weight_ref.shape[1]

    def reorder(g):
        row = g % heads_in_block * queries_count
        weights[g // heads_in_block, row : row + queries_count, :] = weight_ref[:, g : g + 1].astype(F32)
        picked = flat_queries[pl.ds(g, queries_count, stride=index_heads), :]
        idx_q[g // heads_in_block, row : row + queries_count, :] = picked.astype(BF16)

    early = (tiles * 3) // 4
    late = tiles // 2
    share = index_heads // (tiles - late)
    for t in range(tiles):
        if t * tile == half_rows:
            for load in loads[2:]:
                load.wait()
        multiply(t)
        if t == late:
            flat_queries[...] = query_ref[...].astype(F32)
        if t >= late:
            for g in range((t - late) * share, index_heads if t == tiles - 1 else (t - late + 1) * share):
                reorder(g)
        if t:
            soften(t - 1)
        if t == early:
            pl.semaphore_wait(barrier, devices - 1)
            stat_start(0)
    soften(tiles - 1)
    stat_start(1)

    def index_copy(slots, target):
        return pltpu.make_async_remote_copy(
            src_ref=index_all.at[slots],
            dst_ref=index_all.at[slots],
            send_sem=index_send_sem.at[0],
            recv_sem=index_recv_sem.at[0],
            device_id=place(target),
            device_id_type=MESH,
        )

    def index_start(offset, carry):
        index_copy(me, lax.rem(me + offset, devices)).start()
        return carry

    def index_scores(i, logits):
        queries = idx_q[pl.ds(i * group, group)]
        part = lax.dot_general(
            queries.reshape(group * block, -1), keys_ref[...], NT, preferred_element_type=F32
        )
        part = part.reshape(group, block, fine)
        act[pl.ds(i * group, group)] = part
        weighted = weights[pl.ds(i * group, group)] * jnp.maximum(part, 0.0)
        return logits + jnp.sum(
            weighted.reshape(group * heads_in_block, queries_count, fine), axis=0
        )

    logits = lax.fori_loop(
        0, blocks // group, index_scores, jnp.zeros((queries_count, fine), F32)
    )
    index_top = jnp.max(logits, axis=1, keepdims=True)
    index_total = jnp.sum(jnp.exp(logits - index_top), axis=1, keepdims=True)
    index_all[me] = to_row(index_top + jnp.log(index_total))
    lax.fori_loop(1, devices, index_start, 0)

    def sum_copy(half, sources, slots, target):
        return pltpu.make_async_remote_copy(
            src_ref=sum_send.at[half, sources],
            dst_ref=sum_recv.at[half, slots],
            send_sem=sum_send_sem.at[half],
            recv_sem=sum_recv_sem.at[half],
            device_id=(target, my_seq),
            device_id_type=MESH,
        )

    other_heads = pl.ds(0, heads_axis - 1)

    def combine(half, target):
        mine = expo[half, pl.ds(pl.multiple_of(target * fine, fine), fine), :]
        both = lax.dot_general(spread[half], mine, NT, preferred_element_type=F32)
        return both[0:half_queries] + both[half_queries : 2 * half_queries]

    own_parts = []
    for half in range(halves):
        stat_copy(half, other_seqs, my_seq).wait_recv()
        factor = jnp.exp2(base[half] - join_log2(stat_all[half]))
        upper = factor.astype(BF16).astype(F32)
        lower = factor - upper
        first = lax.broadcasted_iota(jnp.int32, (half_queries, 128), 0) * local_heads
        for j in range(half_rows // 128):
            lane = lax.broadcasted_iota(jnp.int32, (half_queries, 128), 1) + j * 128
            inside = jnp.logical_and(lane >= first, lane < first + local_heads)
            columns = slice(j * 128, (j + 1) * 128)
            spread[half, 0:half_queries, columns] = jnp.where(
                inside, upper[j : j + 1, :], 0.0
            ).astype(BF16)
            spread[half, half_queries : 2 * half_queries, columns] = jnp.where(
                inside, lower[j : j + 1, :], 0.0
            ).astype(BF16)
        for offset in range(1, heads_axis):
            target = lax.rem(my_head + offset, heads_axis)
            sum_send[half, target] = combine(half, target)
            sum_copy(half, target, my_head, target).start()
        own_parts.append(combine(half, my_head))

    for half in range(halves):
        sum_copy(half, other_heads, other_heads, my_head).wait_recv()
        for offset in range(1, heads_axis):
            source = lax.rem(my_head + offset, heads_axis)
            own_parts[half] = own_parts[half] + sum_recv[half, source]
    targets = jnp.concatenate(own_parts, axis=0) / heads
    index_copy(other_devices, me).wait_recv()
    index_log = to_column(join_log(index_all[...]), queries_count)
    shifted = logits - index_log
    positive = targets > 0
    own_loss = jnp.where(positive, targets * jnp.log(jnp.where(positive, targets, 1.0)), 0.0)
    own_loss = jnp.sum(own_loss - targets * shifted, axis=0, keepdims=True)
    own_loss = sum(own_loss[:, i * 128 : (i + 1) * 128] for i in range(fine // 128))
    grad = jnp.exp(shifted) - targets
    loss_all[me] = own_loss

    def loss_copy(slots, target):
        return pltpu.make_async_remote_copy(
            src_ref=loss_all.at[slots],
            dst_ref=loss_all.at[slots],
            send_sem=loss_send_sem.at[0],
            recv_sem=loss_recv_sem.at[0],
            device_id=place(target),
            device_id_type=MESH,
        )

    chunk = own_term.shape[1]
    owners = block // chunk
    depth, peers = term_a.shape[0:2]
    inner = seq_axis // depth
    lanes = inner // 2
    my_depth = my_seq // inner
    my_inner = lax.rem(my_seq, inner)
    parity = lax.rem(my_seq, 2)
    pair = my_seq + 1 - 2 * parity
    my_peer = my_head * lanes + my_inner // 2

    def peer_at(offset):
        return lax.rem(my_peer + offset, peers)

    def depth_at(distance):
        return lax.rem(my_depth + distance, depth)

    def owner_of(layer, peer, side):
        return (peer // lanes) * seq_axis + layer * inner + 2 * lax.rem(peer, lanes) + side

    every_peer = pl.ds(0, peers)
    other_peers = pl.ds(0, peers - 1)
    other_layers = pl.ds(0, depth - 1)

    def pair_copy(layer, slots):
        return pltpu.make_async_remote_copy(
            src_ref=own_term.at[slots],
            dst_ref=pair_recv.at[slots],
            send_sem=pair_send_sem.at[0],
            recv_sem=pair_recv_sem.at[layer],
            device_id=(my_head, pair),
            device_id_type=MESH,
        )

    def plane_copy(layer, sources, slots, target):
        return pltpu.make_async_remote_copy(
            src_ref=term_a.at[layer, sources],
            dst_ref=recv_a.at[layer, slots],
            send_sem=a_send_sem.at[layer],
            recv_sem=a_recv_sem.at[layer],
            device_id=(target // lanes, my_depth * inner + 2 * lax.rem(target, lanes) + parity),
            device_id_type=MESH,
        )

    def depth_copy(sources, slots, target):
        return pltpu.make_async_remote_copy(
            src_ref=term_b.at[sources],
            dst_ref=recv_b.at[slots],
            send_sem=b_send_sem.at[0],
            recv_sem=b_recv_sem.at[0],
            device_id=(my_head, target * inner + my_inner),
            device_id_type=MESH,
        )

    grads = jnp.concatenate([grad] * heads_in_block, axis=0)
    grad_upper = grads.astype(BF16).astype(F32)
    grad_lower = grads - grad_upper

    def back(chosen):
        upper_parts, lower_parts = [], []
        for b in chosen:
            part = act[b]
            on = part > 0
            dact[b] = jnp.where(on, grads * weights[b], 0.0).astype(BF16)
            upper_parts.append(jnp.where(on, grad_upper, 0.0).astype(BF16))
            lower_parts.append(jnp.where(on, grad_lower, 0.0).astype(BF16))
        both = jnp.concatenate(upper_parts + lower_parts, axis=0)
        result = jnp.dot(both, keys_ref[...], preferred_element_type=F32)
        result = result[0 : block * len(chosen)] + result[block * len(chosen) :]
        for i, b in enumerate(chosen):
            for j in range(owners):
                start = i * block + j * chunk
                own_term[b * owners + j] = result[start : start + chunk]

    def layer_at(step):
        up = step + jnp.where(step >= my_depth, 1, 0)
        down = depth - 1 - step
        down = down - jnp.where(down <= my_depth, 1, 0)
        return jnp.where(step >= depth - 1, my_depth, jnp.where(2 * my_depth >= depth, up, down))

    def pair_start(layer):
        for offset in range(peers):
            pair_copy(layer, owner_of(layer, peer_at(offset), 1 - parity)).start()

    def plane_start(layer):
        pair_copy(layer, every_peer).wait_recv()
        for offset in range(1, peers):
            peer = peer_at(offset)
            owner = owner_of(layer, peer, parity)
            term_a[layer, peer] = (own_term[owner] + pair_recv[owner]).astype(BF16)
            plane_copy(layer, peer, my_peer, peer).start()

    def layer_back(layer, side):
        if owners == 1:
            back([owner_of(layer, peer_at(offset), side) for offset in range(peers)])

    if owners > 1:

        def every_block(b, carry):
            back([b])
            return carry

        lax.fori_loop(0, blocks, every_block, 0)

    layer_back(layer_at(0), 1 - parity)
    pair_start(layer_at(0))

    def mixed(step, carry):
        ahead = layer_at(step + 1)
        layer_back(ahead, 1 - parity)
        pair_start(ahead)
        layer = layer_at(step)
        layer_back(layer, parity)
        plane_start(layer)
        return carry

    lax.fori_loop(0, depth - 1, mixed, 0)
    layer_back(my_depth, parity)
    plane_start(my_depth)

    def loss_start(offset, carry):
        loss_copy(me, lax.rem(me + offset, devices)).start()
        return carry

    lax.fori_loop(1, devices, loss_start, 0)

    key_out[...] = lax.dot_general(
        dact[...].reshape(blocks * block, fine),
        idx_q[...].reshape(blocks * block, -1),
        TN,
        preferred_element_type=F32,
    )

    for half in range(halves):
        stat_copy(half, other_seqs, my_seq).wait_send()
        sum_copy(half, other_heads, other_heads, my_head).wait_send()
    index_copy(other_devices, me).wait_send()

    pair_copy(0, pl.ds(0, depth * peers)).wait_send()

    def plane_total(layer):
        owner = owner_of(layer, my_peer, parity)
        plane_copy(layer, other_peers, other_peers, my_peer).wait_recv()
        total = own_term[owner] + pair_recv[owner]
        for offset in range(1, peers):
            total = total + recv_a[layer, peer_at(offset)].astype(F32)
        return total

    def depth_start(step, carry):
        layer = layer_at(step)
        term_b[layer] = plane_total(layer).astype(BF16)
        depth_copy(layer, my_depth, layer).start()
        return carry

    lax.fori_loop(0, depth - 1, depth_start, 0)
    total = plane_total(my_depth)
    if depth > 1:
        depth_copy(other_layers, other_layers, my_depth).wait_recv()
    for distance in range(1, depth):
        total = total + recv_b[depth_at(distance)].astype(F32)
    own_block = me // owners
    inside_block = me - own_block * owners
    own_weights = weights[own_block]
    own_queries = idx_q[own_block].astype(F32)
    if owners == 1:
        query_out[...] = total * own_weights
        prod_out[...] = total * own_queries
    else:
        for j in range(owners):

            @pl.when(inside_block == j)
            def _():
                query_out[...] = total * own_weights[j * chunk : (j + 1) * chunk]
                prod_out[...] = total * own_queries[j * chunk : (j + 1) * chunk]

    loss_copy(other_devices, me).wait_recv()
    loss_out[...] = jnp.sum(loss_all[...], axis=0)
    loss_copy(other_devices, me).wait_send()

    def plane_sent(layer, carry):
        plane_copy(layer, other_peers, other_peers, my_peer).wait_send()
        return carry

    lax.fori_loop(0, depth, plane_sent, 0)
    if depth > 1:
        depth_copy(other_layers, other_layers, my_depth).wait_send()


def closing(queries_count, loss_in, query_in, prod_in, key_in, loss_out, query_out, weight_out, key_out):
    loss_out[...] = jnp.sum(loss_in[...], axis=1, keepdims=True) / queries_count
    query_out[...] = query_in[...]
    ones = jnp.ones((8, prod_in.shape[1]), F32)
    sums = lax.dot_general(
        ones, prod_in[...], NT, precision=lax.Precision.HIGHEST, preferred_element_type=F32
    )
    weight_out[...] = sums[0:1]
    key_out[...] = key_in[...]


def shards(heads_axis, seq_axis, latent_q, latent_keys, idx_q, idx_keys, idx_weight):
    queries_count, local_heads, width = latent_q.shape
    index_heads, size = idx_q.shape[1:]
    rows = queries_count * local_heads
    keys = latent_keys.shape[0]
    fine = idx_keys.shape[1]
    devices = heads_axis * seq_axis
    all_rows = queries_count * index_heads
    chunk = all_rows // devices
    block = max(chunk, queries_count)
    blocks = all_rows // block
    halves = 2
    half_rows = rows // halves
    half_queries = queries_count // halves
    tile = min(256, half_rows)
    inner = math.gcd(seq_axis, 4)
    depth = seq_axis // inner
    peers = heads_axis * inner // 2
    queries = idx_q.reshape(all_rows, size)
    vmem = pl.BlockSpec(memory_space=pltpu.VMEM)
    dma = pltpu.SemaphoreType.DMA
    loss, query_grad, prod, key_grad = pl.pallas_call(
        functools.partial(
            kernel, heads_axis, seq_axis, local_heads * heads_axis, queries_count
        ),
        out_shape=(
            jax.ShapeDtypeStruct((1, 128), F32),
            jax.ShapeDtypeStruct((chunk, size), F32),
            jax.ShapeDtypeStruct((chunk, size), F32),
            jax.ShapeDtypeStruct((fine, size), F32),
        ),
        in_specs=[pl.BlockSpec(memory_space=pl.ANY)] * 5,
        out_specs=(vmem,) * 4,
        scratch_shapes=[
            pltpu.VMEM((rows, width), BF16),
            pltpu.VMEM((width, keys), BF16),
            pltpu.VMEM((all_rows, size), BF16),
            pltpu.VMEM((fine, size), BF16),
            pltpu.VMEM((queries_count, index_heads), BF16),
            dma((halves + 4,)),
            pltpu.VMEM((keys, width), BF16),
            pltpu.VMEM((keys, tile), F32),
            pltpu.VMEM((keys, tile), F32),
            pltpu.VMEM((1, tile), F32),
            pltpu.VMEM((1, tile), F32),
            pltpu.VMEM((blocks, block, size), BF16),
            pltpu.VMEM((all_rows, size), F32),
            pltpu.VMEM((blocks, block, 1), F32),
            pltpu.VMEM((devices, chunk, size), F32),
            pltpu.VMEM((devices, chunk, size), F32),
            pltpu.VMEM((devices, 1, 128), F32),
            pltpu.VMEM((halves, keys, half_rows), BF16),
            pltpu.VMEM((halves, half_rows // 128, 128), F32),
            pltpu.VMEM((halves, 2 * half_queries, half_rows), BF16),
            pltpu.VMEM((halves, seq_axis, half_rows // 128, 128), F32),
            pltpu.VMEM((halves, heads_axis, half_queries, fine), F32),
            pltpu.VMEM((halves, heads_axis, half_queries, fine), F32),
            pltpu.VMEM((blocks, block, fine), F32),
            pltpu.VMEM((blocks, block, fine), BF16),
            pltpu.VMEM((depth, peers, chunk, size), BF16),
            pltpu.VMEM((depth, peers, chunk, size), BF16),
            pltpu.VMEM((depth, chunk, size), BF16),
            pltpu.VMEM((depth, chunk, size), BF16),
            pltpu.VMEM((devices, 1, 128), F32),
            dma((halves,)),
            dma((halves,)),
            dma((halves,)),
            dma((halves,)),
            dma((depth,)),
            dma((depth,)),
            dma((1,)),
            dma((1,)),
            dma((1,)),
            dma((1,)),
            dma((1,)),
            dma((depth,)),
            dma((1,)),
            dma((1,)),
        ],
        compiler_params=pltpu.CompilerParams(
            collective_id=0, has_side_effects=True, vmem_limit_bytes=60 * 1024 * 1024
        ),
    )(latent_q.reshape(rows, width), latent_keys.T, queries, idx_keys[0], idx_weight)
    loss, query_grad, weight_grad, key_grad = pl.pallas_call(
        functools.partial(closing, queries_count),
        out_shape=(
            jax.ShapeDtypeStruct((1, 1), F32),
            jax.ShapeDtypeStruct((chunk, size), F32),
            jax.ShapeDtypeStruct((1, chunk), F32),
            jax.ShapeDtypeStruct((fine, size), F32),
        ),
        in_specs=[vmem] * 4,
        out_specs=(vmem,) * 4,
    )(loss, query_grad, prod, key_grad)
    return (loss.reshape(()), query_grad, weight_grad.reshape(-1), key_grad[None])


def solution(mesh):
    in_specs = (P(None, "head", None), P("seq", None), P(), P("seq", "head", None), P())
    out_specs = (P(), P(("head", "seq"), None), P(("head", "seq")), P("seq", "head", None))
    body = functools.partial(shards, mesh.shape["head"], mesh.shape["seq"])
    return jax.shard_map(body, mesh=mesh, in_specs=in_specs, out_specs=out_specs, check_vma=False)
```

```python
import functools
import math

import jax
import jax.numpy as jnp
from jax import lax
from jax.experimental import pallas as pl
from jax.experimental.pallas import tpu as pltpu
from jax.sharding import PartitionSpec as P

MESH = pl.DeviceIdType.MESH
NT = (((1,), (1,)), ((), ()))
TN = (((0,), (0,)), ((), ()))
F32 = jnp.float32
BF16 = jnp.bfloat16

exponent_scale = 192 ** (-0.5) * math.log2(math.e)


def to_row(column):
    wide = jnp.broadcast_to(column, (column.shape[0], 128))
    copies = 128 // column.shape[0]
    return jnp.concatenate([wide] * copies, axis=0).T[0:1, :]


def to_column(row, count):
    return jnp.broadcast_to(row, (128, 128)).T[0:count, 0:1]


def join_log2(values):
    top = jnp.max(values, axis=0)
    return top + jnp.log2(jnp.sum(jnp.exp2(values - top[None]), axis=0))


def join_log(values):
    top = jnp.max(values, axis=0)
    return top + jnp.log(jnp.sum(jnp.exp(values - top[None]), axis=0))


def kernel(
    heads_axis, seq_axis, heads, queries_count,
    latent_q_hbm, turned_keys_hbm, query_hbm, keys_hbm, weight_hbm,
    loss_out, query_out, prod_out, key_out,
    latent_q, turned_keys, query_ref, keys_ref, weight_ref, load_sem,
    latent_keys, scores_a, scores_b, top_a, top_b,
    idx_q, flat_queries, weights, own_term, pair_recv, index_all, expo, base, spread, stat_all, sum_send, sum_recv, act, dact, term_a, recv_a, term_b, recv_b, loss_all,
    stat_send_sem, stat_recv_sem, sum_send_sem, sum_recv_sem,
    a_send_sem, a_recv_sem, b_send_sem, b_recv_sem, loss_send_sem, loss_recv_sem, pair_send_sem, pair_recv_sem, index_send_sem, index_recv_sem,
):
    my_head = lax.axis_index("head")
    my_seq = lax.axis_index("seq")
    devices = heads_axis * seq_axis
    me = my_head * seq_axis + my_seq
    barrier = pltpu.get_barrier_semaphore()
    rows, width = latent_q.shape
    local_heads = rows // queries_count
    halves, _, half_rows = expo.shape
    half_queries = queries_count // halves
    tile = top_a.shape[1]
    tiles = rows // tile

    def place(index):
        return (index // seq_axis, lax.rem(index, seq_axis))

    loads = [pltpu.make_async_copy(turned_keys_hbm, turned_keys, load_sem.at[0])]
    for j in range(halves):
        part = pl.ds(j * half_rows, half_rows)
        loads.append(pltpu.make_async_copy(latent_q_hbm.at[part], latent_q.at[part], load_sem.at[1 + j]))
    loads.append(pltpu.make_async_copy(query_hbm, query_ref, load_sem.at[halves + 1]))
    loads.append(pltpu.make_async_copy(keys_hbm, keys_ref, load_sem.at[halves + 2]))
    loads.append(pltpu.make_async_copy(weight_hbm, weight_ref, load_sem.at[halves + 3]))
    for load in loads:
        load.start()

    def greet(offset, carry):
        other = lax.rem(me + offset, devices)
        pl.semaphore_signal(barrier, inc=1, device_id=place(other), device_id_type=MESH)
        return carry

    lax.fori_loop(1, devices, greet, 0)

    def stat_copy(half, slots, target):
        return pltpu.make_async_remote_copy(
            src_ref=stat_all.at[half, slots],
            dst_ref=stat_all.at[half, slots],
            send_sem=stat_send_sem.at[half],
            recv_sem=stat_recv_sem.at[half],
            device_id=(my_head, target),
            device_id_type=MESH,
        )

    def stat_start(half):
        def start(offset, carry):
            stat_copy(half, my_seq, lax.rem(my_seq + offset, seq_axis)).start()
            return carry

        lax.fori_loop(1, seq_axis, start, 0)

    other_seqs = pl.ds(0, seq_axis - 1)
    other_devices = pl.ds(0, devices - 1)

    loads[0].wait()
    latent_keys[...] = turned_keys[...].T
    loads[1].wait()
    buffers = [(scores_a, top_a), (scores_b, top_b)]

    def multiply(t):
        buffer, top = buffers[t % 2]
        scores = lax.dot_general(
            latent_keys[...], latent_q[pl.ds(t * tile, tile), :], NT, preferred_element_type=F32
        )
        buffer[...] = scores
        top[...] = jnp.max(scores, axis=0, keepdims=True)

    def soften(t):
        buffer, top_ref = buffers[t % 2]
        top = top_ref[...]
        part = jnp.exp2((buffer[...] - top) * exponent_scale)
        half = t * tile // half_rows
        start = t * tile - half * half_rows
        expo[half, :, start : start + tile] = part.astype(BF16)
        total = jnp.sum(part, axis=0, keepdims=True)
        scaled = top * exponent_scale
        joint = scaled + jnp.log2(total)
        for j in range(tile // 128):
            row = start // 128 + j
            base[half, row : row + 1, :] = scaled[:, j * 128 : (j + 1) * 128]
            stat_all[half, my_seq, row : row + 1, :] = joint[:, j * 128 : (j + 1) * 128]

    blocks, block, _ = weights.shape
    fine = keys_ref.shape[0]
    group = math.gcd(blocks, 8)
    heads_in_block = block // queries_count
    index_heads = weight_ref.shape[1]

    def reorder(g):
        row = g % heads_in_block * queries_count
        weights[g // heads_in_block, row : row + queries_count, :] = weight_ref[:, g : g + 1].astype(F32)
        picked = flat_queries[pl.ds(g, queries_count, stride=index_heads), :]
        idx_q[g // heads_in_block, row : row + queries_count, :] = picked.astype(BF16)

    early = (tiles * 5) // 8
    late = tiles // 2
    share = index_heads // (tiles - late)
    for t in range(tiles):
        if t * tile == half_rows:
            for load in loads[2:]:
                load.wait()
        multiply(t)
        if t == late:
            flat_queries[...] = query_ref[...].astype(F32)
        if t >= late:
            for g in range((t - late) * share, index_heads if t == tiles - 1 else (t - late + 1) * share):
                reorder(g)
        if t:
            soften(t - 1)
        if t == early:
            pl.semaphore_wait(barrier, devices - 1)
            stat_start(0)
    soften(tiles - 1)
    stat_start(1)

    def index_copy(slots, target):
        return pltpu.make_async_remote_copy(
            src_ref=index_all.at[slots],
            dst_ref=index_all.at[slots],
            send_sem=index_send_sem.at[0],
            recv_sem=index_recv_sem.at[0],
            device_id=place(target),
            device_id_type=MESH,
        )

    def index_start(offset, carry):
        index_copy(me, lax.rem(me + offset, devices)).start()
        return carry

    def index_scores(i, logits):
        queries = idx_q[pl.ds(i * group, group)]
        part = lax.dot_general(
            queries.reshape(group * block, -1), keys_ref[...], NT, preferred_element_type=F32
        )
        part = part.reshape(group, block, fine)
        act[pl.ds(i * group, group)] = part
        weighted = weights[pl.ds(i * group, group)] * jnp.maximum(part, 0.0)
        return logits + jnp.sum(
            weighted.reshape(group * heads_in_block, queries_count, fine), axis=0
        )

    logits = lax.fori_loop(
        0, blocks // group, index_scores, jnp.zeros((queries_count, fine), F32)
    )
    index_top = jnp.max(logits, axis=1, keepdims=True)
    index_total = jnp.sum(jnp.exp(logits - index_top), axis=1, keepdims=True)
    index_all[me] = to_row(index_top + jnp.log(index_total))
    lax.fori_loop(1, devices, index_start, 0)

    def sum_copy(half, sources, slots, target):
        return pltpu.make_async_remote_copy(
            src_ref=sum_send.at[half, sources],
            dst_ref=sum_recv.at[half, slots],
            send_sem=sum_send_sem.at[half],
            recv_sem=sum_recv_sem.at[half],
            device_id=(target, my_seq),
            device_id_type=MESH,
        )

    other_heads = pl.ds(0, heads_axis - 1)

    def combine(half, target):
        mine = expo[half, pl.ds(pl.multiple_of(target * fine, fine), fine), :]
        both = lax.dot_general(spread[half], mine, NT, preferred_element_type=F32)
        return both[0:half_queries] + both[half_queries : 2 * half_queries]

    own_parts = []
    for half in range(halves):
        stat_copy(half, other_seqs, my_seq).wait_recv()
        factor = jnp.exp2(base[half] - join_log2(stat_all[half]))
        upper = factor.astype(BF16).astype(F32)
        lower = factor - upper
        first = lax.broadcasted_iota(jnp.int32, (half_queries, 128), 0) * local_heads
        for j in range(half_rows // 128):
            lane = lax.broadcasted_iota(jnp.int32, (half_queries, 128), 1) + j * 128
            inside = jnp.logical_and(lane >= first, lane < first + local_heads)
            columns = slice(j * 128, (j + 1) * 128)
            spread[half, 0:half_queries, columns] = jnp.where(
                inside, upper[j : j + 1, :], 0.0
            ).astype(BF16)
            spread[half, half_queries : 2 * half_queries, columns] = jnp.where(
                inside, lower[j : j + 1, :], 0.0
            ).astype(BF16)
        for offset in range(1, heads_axis):
            target = lax.rem(my_head + offset, heads_axis)
            sum_send[half, target] = combine(half, target)
            sum_copy(half, target, my_head, target).start()
        own_parts.append(combine(half, my_head))

    for half in range(halves):
        sum_copy(half, other_heads, other_heads, my_head).wait_recv()
        for offset in range(1, heads_axis):
            source = lax.rem(my_head + offset, heads_axis)
            own_parts[half] = own_parts[half] + sum_recv[half, source]
    targets = jnp.concatenate(own_parts, axis=0) / heads
    index_copy(other_devices, me).wait_recv()
    index_log = to_column(join_log(index_all[...]), queries_count)
    shifted = logits - index_log
    positive = targets > 0
    own_loss = jnp.where(positive, targets * jnp.log(jnp.where(positive, targets, 1.0)), 0.0)
    own_loss = jnp.sum(own_loss - targets * shifted, axis=0, keepdims=True)
    own_loss = sum(own_loss[:, i * 128 : (i + 1) * 128] for i in range(fine // 128))
    grad = jnp.exp(shifted) - targets
    loss_all[me] = own_loss

    def loss_copy(slots, target):
        return pltpu.make_async_remote_copy(
            src_ref=loss_all.at[slots],
            dst_ref=loss_all.at[slots],
            send_sem=loss_send_sem.at[0],
            recv_sem=loss_recv_sem.at[0],
            device_id=place(target),
            device_id_type=MESH,
        )

    chunk = own_term.shape[1]
    owners = block // chunk
    depth, peers = term_a.shape[0:2]
    inner = seq_axis // depth
    lanes = inner // 2
    my_depth = my_seq // inner
    my_inner = lax.rem(my_seq, inner)
    parity = lax.rem(my_seq, 2)
    pair = my_seq + 1 - 2 * parity
    my_peer = my_head * lanes + my_inner // 2

    def peer_at(offset):
        return lax.rem(my_peer + offset, peers)

    def depth_at(distance):
        return lax.rem(my_depth + distance, depth)

    def owner_of(layer, peer, side):
        return (peer // lanes) * seq_axis + layer * inner + 2 * lax.rem(peer, lanes) + side

    every_peer = pl.ds(0, peers)
    other_peers = pl.ds(0, peers - 1)
    other_layers = pl.ds(0, depth - 1)

    def pair_copy(layer, slots):
        return pltpu.make_async_remote_copy(
            src_ref=own_term.at[slots],
            dst_ref=pair_recv.at[slots],
            send_sem=pair_send_sem.at[0],
            recv_sem=pair_recv_sem.at[layer],
            device_id=(my_head, pair),
            device_id_type=MESH,
        )

    def plane_copy(layer, sources, slots, target):
        return pltpu.make_async_remote_copy(
            src_ref=term_a.at[layer, sources],
            dst_ref=recv_a.at[layer, slots],
            send_sem=a_send_sem.at[layer],
            recv_sem=a_recv_sem.at[layer],
            device_id=(target // lanes, my_depth * inner + 2 * lax.rem(target, lanes) + parity),
            device_id_type=MESH,
        )

    def depth_copy(sources, slots, target):
        return pltpu.make_async_remote_copy(
            src_ref=term_b.at[sources],
            dst_ref=recv_b.at[slots],
            send_sem=b_send_sem.at[0],
            recv_sem=b_recv_sem.at[0],
            device_id=(my_head, target * inner + my_inner),
            device_id_type=MESH,
        )

    grads = jnp.concatenate([grad] * heads_in_block, axis=0)
    grad_upper = grads.astype(BF16).astype(F32)
    grad_lower = grads - grad_upper

    def back(chosen):
        upper_parts, lower_parts = [], []
        for b in chosen:
            part = act[b]
            on = part > 0
            dact[b] = jnp.where(on, grads * weights[b], 0.0).astype(BF16)
            upper_parts.append(jnp.where(on, grad_upper, 0.0).astype(BF16))
            lower_parts.append(jnp.where(on, grad_lower, 0.0).astype(BF16))
        both = jnp.concatenate(upper_parts + lower_parts, axis=0)
        result = jnp.dot(both, keys_ref[...], preferred_element_type=F32)
        result = result[0 : block * len(chosen)] + result[block * len(chosen) :]
        for i, b in enumerate(chosen):
            for j in range(owners):
                start = i * block + j * chunk
                own_term[b * owners + j] = result[start : start + chunk]

    def layer_at(step):
        up = step + jnp.where(step >= my_depth, 1, 0)
        down = depth - 1 - step
        down = down - jnp.where(down <= my_depth, 1, 0)
        return jnp.where(step >= depth - 1, my_depth, jnp.where(2 * my_depth >= depth, up, down))

    def pair_start(layer):
        for offset in range(peers):
            pair_copy(layer, owner_of(layer, peer_at(offset), 1 - parity)).start()

    def plane_start(layer):
        pair_copy(layer, every_peer).wait_recv()
        for offset in range(1, peers):
            peer = peer_at(offset)
            owner = owner_of(layer, peer, parity)
            term_a[layer, peer] = (own_term[owner] + pair_recv[owner]).astype(BF16)
            plane_copy(layer, peer, my_peer, peer).start()

    def layer_back(layer, side):
        if owners == 1:
            back([owner_of(layer, peer_at(offset), side) for offset in range(peers)])

    if owners > 1:

        def every_block(b, carry):
            back([b])
            return carry

        lax.fori_loop(0, blocks, every_block, 0)

    layer_back(layer_at(0), 1 - parity)
    pair_start(layer_at(0))

    def mixed(step, carry):
        ahead = layer_at(step + 1)
        layer_back(ahead, 1 - parity)
        pair_start(ahead)
        layer = layer_at(step)
        layer_back(layer, parity)
        plane_start(layer)
        return carry

    lax.fori_loop(0, depth - 1, mixed, 0)
    layer_back(my_depth, parity)
    plane_start(my_depth)

    def loss_start(offset, carry):
        loss_copy(me, lax.rem(me + offset, devices)).start()
        return carry

    lax.fori_loop(1, devices, loss_start, 0)

    key_out[...] = lax.dot_general(
        dact[...].reshape(blocks * block, fine),
        idx_q[...].reshape(blocks * block, -1),
        TN,
        preferred_element_type=F32,
    )

    for half in range(halves):
        stat_copy(half, other_seqs, my_seq).wait_send()
        sum_copy(half, other_heads, other_heads, my_head).wait_send()
    index_copy(other_devices, me).wait_send()

    pair_copy(0, pl.ds(0, depth * peers)).wait_send()

    def plane_total(layer):
        owner = owner_of(layer, my_peer, parity)
        plane_copy(layer, other_peers, other_peers, my_peer).wait_recv()
        total = own_term[owner] + pair_recv[owner]
        for offset in range(1, peers):
            total = total + recv_a[layer, peer_at(offset)].astype(F32)
        return total

    def depth_start(step, carry):
        layer = layer_at(step)
        term_b[layer] = plane_total(layer).astype(BF16)
        depth_copy(layer, my_depth, layer).start()
        return carry

    lax.fori_loop(0, depth - 1, depth_start, 0)
    total = plane_total(my_depth)
    if depth > 1:
        depth_copy(other_layers, other_layers, my_depth).wait_recv()
    for distance in range(1, depth):
        total = total + recv_b[depth_at(distance)].astype(F32)
    own_block = me // owners
    inside_block = me - own_block * owners
    own_weights = weights[own_block]
    own_queries = idx_q[own_block].astype(F32)
    if owners == 1:
        query_out[...] = total * own_weights
        prod_out[...] = total * own_queries
    else:
        for j in range(owners):

            @pl.when(inside_block == j)
            def _():
                query_out[...] = total * own_weights[j * chunk : (j + 1) * chunk]
                prod_out[...] = total * own_queries[j * chunk : (j + 1) * chunk]

    loss_copy(other_devices, me).wait_recv()
    loss_out[...] = jnp.sum(loss_all[...], axis=0)
    loss_copy(other_devices, me).wait_send()

    def plane_sent(layer, carry):
        plane_copy(layer, other_peers, other_peers, my_peer).wait_send()
        return carry

    lax.fori_loop(0, depth, plane_sent, 0)
    if depth > 1:
        depth_copy(other_layers, other_layers, my_depth).wait_send()


def closing(queries_count, loss_in, query_in, prod_in, key_in, loss_out, query_out, weight_out, key_out, sems):
    copies = [
        pltpu.make_async_copy(key_in, key_out, sems.at[0]),
        pltpu.make_async_copy(query_in, query_out, sems.at[1]),
    ]
    for copy in copies:
        copy.start()
    loss_out[...] = jnp.sum(loss_in[...], axis=1, keepdims=True) / queries_count
    ones = jnp.ones((8, prod_in.shape[1]), F32)
    sums = lax.dot_general(
        ones, prod_in[...], NT, precision=lax.Precision.HIGHEST, preferred_element_type=F32
    )
    weight_out[...] = sums[0:1]
    for copy in copies:
        copy.wait()


def shards(heads_axis, seq_axis, latent_q, latent_keys, idx_q, idx_keys, idx_weight):
    queries_count, local_heads, width = latent_q.shape
    index_heads, size = idx_q.shape[1:]
    rows = queries_count * local_heads
    keys = latent_keys.shape[0]
    fine = idx_keys.shape[1]
    devices = heads_axis * seq_axis
    all_rows = queries_count * index_heads
    chunk = all_rows // devices
    block = max(chunk, queries_count)
    blocks = all_rows // block
    halves = 2
    half_rows = rows // halves
    half_queries = queries_count // halves
    tile = min(256, half_rows)
    inner = math.gcd(seq_axis, 4)
    depth = seq_axis // inner
    peers = heads_axis * inner // 2
    queries = idx_q.reshape(all_rows, size)
    vmem = pl.BlockSpec(memory_space=pltpu.VMEM)
    dma = pltpu.SemaphoreType.DMA
    loss, query_grad, prod, key_grad = pl.pallas_call(
        functools.partial(
            kernel, heads_axis, seq_axis, local_heads * heads_axis, queries_count
        ),
        out_shape=(
            pltpu.VMEM((1, 128), F32),
            pltpu.VMEM((chunk, size), F32),
            pltpu.VMEM((chunk, size), F32),
            pltpu.VMEM((fine, size), F32),
        ),
        in_specs=[pl.BlockSpec(memory_space=pltpu.HBM)] * 5,
        out_specs=(vmem,) * 4,
        scratch_shapes=[
            pltpu.VMEM((rows, width), BF16),
            pltpu.VMEM((width, keys), BF16),
            pltpu.VMEM((all_rows, size), BF16),
            pltpu.VMEM((fine, size), BF16),
            pltpu.VMEM((queries_count, index_heads), BF16),
            dma((halves + 4,)),
            pltpu.VMEM((keys, width), BF16),
            pltpu.VMEM((keys, tile), F32),
            pltpu.VMEM((keys, tile), F32),
            pltpu.VMEM((1, tile), F32),
            pltpu.VMEM((1, tile), F32),
            pltpu.VMEM((blocks, block, size), BF16),
            pltpu.VMEM((all_rows, size), F32),
            pltpu.VMEM((blocks, block, 1), F32),
            pltpu.VMEM((devices, chunk, size), F32),
            pltpu.VMEM((devices, chunk, size), F32),
            pltpu.VMEM((devices, 1, 128), F32),
            pltpu.VMEM((halves, keys, half_rows), BF16),
            pltpu.VMEM((halves, half_rows // 128, 128), F32),
            pltpu.VMEM((halves, 2 * half_queries, half_rows), BF16),
            pltpu.VMEM((halves, seq_axis, half_rows // 128, 128), F32),
            pltpu.VMEM((halves, heads_axis, half_queries, fine), F32),
            pltpu.VMEM((halves, heads_axis, half_queries, fine), F32),
            pltpu.VMEM((blocks, block, fine), F32),
            pltpu.VMEM((blocks, block, fine), BF16),
            pltpu.VMEM((depth, peers, chunk, size), BF16),
            pltpu.VMEM((depth, peers, chunk, size), BF16),
            pltpu.VMEM((depth, chunk, size), BF16),
            pltpu.VMEM((depth, chunk, size), BF16),
            pltpu.VMEM((devices, 1, 128), F32),
            dma((halves,)),
            dma((halves,)),
            dma((halves,)),
            dma((halves,)),
            dma((depth,)),
            dma((depth,)),
            dma((1,)),
            dma((1,)),
            dma((1,)),
            dma((1,)),
            dma((1,)),
            dma((depth,)),
            dma((1,)),
            dma((1,)),
        ],
        compiler_params=pltpu.CompilerParams(
            collective_id=0, has_side_effects=True, vmem_limit_bytes=56 * 1024 * 1024
        ),
    )(latent_q.reshape(rows, width), latent_keys.T, queries, idx_keys[0], idx_weight)
    held = [
        pltpu.with_memory_space_constraint(x, pltpu.VMEM)
        for x in (loss, query_grad, prod, key_grad)
    ]
    hbm = pl.BlockSpec(memory_space=pltpu.HBM)
    loss, query_grad, weight_grad, key_grad = pl.pallas_call(
        functools.partial(closing, queries_count),
        out_shape=(
            jax.ShapeDtypeStruct((1, 1), F32),
            jax.ShapeDtypeStruct((chunk, size), F32),
            jax.ShapeDtypeStruct((1, chunk), F32),
            jax.ShapeDtypeStruct((fine, size), F32),
        ),
        in_specs=[vmem] * 4,
        out_specs=(vmem, hbm, vmem, hbm),
        scratch_shapes=[dma((2,))],
    )(*held)
    return (loss.reshape(()), query_grad, weight_grad.reshape(-1), key_grad[None])


def solution(mesh):
    in_specs = (P(None, "head", None), P("seq", None), P(), P("seq", "head", None), P())
    out_specs = (P(), P(("head", "seq"), None), P(("head", "seq")), P("seq", "head", None))
    body = functools.partial(shards, mesh.shape["head"], mesh.shape["seq"])
    return jax.shard_map(body, mesh=mesh, in_specs=in_specs, out_specs=out_specs, check_vma=False)
```

```python
import functools
import math

import jax
import jax.numpy as jnp
from jax import lax
from jax.experimental import pallas as pl
from jax.experimental.pallas import tpu as pltpu
from jax.sharding import PartitionSpec as P

MESH = pl.DeviceIdType.MESH
NT = (((1,), (1,)), ((), ()))
TN = (((0,), (0,)), ((), ()))
F32 = jnp.float32
BF16 = jnp.bfloat16

exponent_scale = 192 ** (-0.5) * math.log2(math.e)


def to_row(column):
    wide = jnp.broadcast_to(column, (column.shape[0], 128))
    copies = 128 // column.shape[0]
    return jnp.concatenate([wide] * copies, axis=0).T[0:1, :]


def to_column(row, count):
    return jnp.broadcast_to(row, (128, 128)).T[0:count, 0:1]


def join_log2(values):
    top = jnp.max(values, axis=0)
    return top + jnp.log2(jnp.sum(jnp.exp2(values - top[None]), axis=0))


def join_log(values):
    top = jnp.max(values, axis=0)
    return top + jnp.log(jnp.sum(jnp.exp(values - top[None]), axis=0))


def kernel(
    heads_axis, seq_axis, heads, queries_count,
    latent_q_hbm, turned_keys_hbm, query_hbm, keys_hbm, weight_hbm,
    loss_out, query_out, prod_out, key_out,
    latent_q, turned_keys, query_ref, keys_ref, weight_ref, load_sem,
    latent_keys, scores_a, scores_b, top_a, top_b,
    idx_q, flat_queries, weights, own_term, pair_recv, index_all, expo, base, spread, stat_all, sum_send, sum_recv, act, dact, term_a, recv_a, term_b, recv_b, loss_all,
    stat_send_sem, stat_recv_sem, sum_send_sem, sum_recv_sem,
    a_send_sem, a_recv_sem, b_send_sem, b_recv_sem, loss_send_sem, loss_recv_sem, pair_send_sem, pair_recv_sem, index_send_sem, index_recv_sem,
):
    my_head = lax.axis_index("head")
    my_seq = lax.axis_index("seq")
    devices = heads_axis * seq_axis
    me = my_head * seq_axis + my_seq
    barrier = pltpu.get_barrier_semaphore()
    rows, width = latent_q.shape
    local_heads = rows // queries_count
    halves, _, half_rows = expo.shape
    half_queries = queries_count // halves
    tile = top_a.shape[1]
    tiles = rows // tile

    def place(index):
        return (index // seq_axis, lax.rem(index, seq_axis))

    loads = [pltpu.make_async_copy(turned_keys_hbm, turned_keys, load_sem.at[0])]
    for j in range(halves):
        part = pl.ds(j * half_rows, half_rows)
        loads.append(pltpu.make_async_copy(latent_q_hbm.at[part], latent_q.at[part], load_sem.at[1 + j]))
    loads.append(pltpu.make_async_copy(query_hbm, query_ref, load_sem.at[halves + 1]))
    loads.append(pltpu.make_async_copy(keys_hbm, keys_ref, load_sem.at[halves + 2]))
    loads.append(pltpu.make_async_copy(weight_hbm, weight_ref, load_sem.at[halves + 3]))
    for load in loads[:2]:
        load.start()

    def greet(offset, carry):
        other = lax.rem(me + offset, devices)
        pl.semaphore_signal(barrier, inc=1, device_id=place(other), device_id_type=MESH)
        return carry

    lax.fori_loop(1, devices, greet, 0)
    for load in loads[2:]:
        load.start()

    def stat_copy(half, slots, target):
        return pltpu.make_async_remote_copy(
            src_ref=stat_all.at[half, slots],
            dst_ref=stat_all.at[half, slots],
            send_sem=stat_send_sem.at[half],
            recv_sem=stat_recv_sem.at[half],
            device_id=(my_head, target),
            device_id_type=MESH,
        )

    def stat_start(half):
        def start(offset, carry):
            stat_copy(half, my_seq, lax.rem(my_seq + offset, seq_axis)).start()
            return carry

        lax.fori_loop(1, seq_axis, start, 0)

    other_seqs = pl.ds(0, seq_axis - 1)
    other_devices = pl.ds(0, devices - 1)

    loads[0].wait()
    latent_keys[...] = turned_keys[...].T
    loads[1].wait()
    buffers = [(scores_a, top_a), (scores_b, top_b)]

    def multiply(t):
        buffer, top = buffers[t % 2]
        scores = lax.dot_general(
            latent_keys[...], latent_q[pl.ds(t * tile, tile), :], NT, preferred_element_type=F32
        )
        buffer[...] = scores
        top[...] = jnp.max(scores, axis=0, keepdims=True)

    def soften(t):
        buffer, top_ref = buffers[t % 2]
        top = top_ref[...]
        part = jnp.exp2((buffer[...] - top) * exponent_scale)
        half = t * tile // half_rows
        start = t * tile - half * half_rows
        expo[half, :, start : start + tile] = part.astype(BF16)
        total = jnp.sum(part, axis=0, keepdims=True)
        scaled = top * exponent_scale
        joint = scaled + jnp.log2(total)
        for j in range(tile // 128):
            row = start // 128 + j
            base[half, row : row + 1, :] = scaled[:, j * 128 : (j + 1) * 128]
            stat_all[half, my_seq, row : row + 1, :] = joint[:, j * 128 : (j + 1) * 128]

    blocks, block, _ = weights.shape
    fine = keys_ref.shape[0]
    group = math.gcd(blocks, 8)
    heads_in_block = block // queries_count
    index_heads = weight_ref.shape[1]

    def reorder(g):
        row = g % heads_in_block * queries_count
        weights[g // heads_in_block, row : row + queries_count, :] = weight_ref[:, g : g + 1].astype(F32)
        picked = flat_queries[pl.ds(g, queries_count, stride=index_heads), :]
        idx_q[g // heads_in_block, row : row + queries_count, :] = picked.astype(BF16)

    early = (tiles * 5) // 8
    late = tiles // 2
    share = index_heads // (tiles - late)
    for t in range(tiles):
        if t * tile == half_rows:
            for load in loads[2:]:
                load.wait()
        multiply(t)
        if t == late:
            flat_queries[...] = query_ref[...].astype(F32)
        if t >= late:
            for g in range((t - late) * share, index_heads if t == tiles - 1 else (t - late + 1) * share):
                reorder(g)
        if t:
            soften(t - 1)
        if t == early:
            pl.semaphore_wait(barrier, devices - 1)
            stat_start(0)
    soften(tiles - 1)
    stat_start(1)

    def index_copy(slots, target):
        return pltpu.make_async_remote_copy(
            src_ref=index_all.at[slots],
            dst_ref=index_all.at[slots],
            send_sem=index_send_sem.at[0],
            recv_sem=index_recv_sem.at[0],
            device_id=place(target),
            device_id_type=MESH,
        )

    def index_start(offset, carry):
        index_copy(me, lax.rem(me + offset, devices)).start()
        return carry

    def index_scores(i, logits):
        queries = idx_q[pl.ds(i * group, group)]
        part = lax.dot_general(
            queries.reshape(group * block, -1), keys_ref[...], NT, preferred_element_type=F32
        )
        part = part.reshape(group, block, fine)
        act[pl.ds(i * group, group)] = part
        weighted = weights[pl.ds(i * group, group)] * jnp.maximum(part, 0.0)
        return logits + jnp.sum(
            weighted.reshape(group * heads_in_block, queries_count, fine), axis=0
        )

    logits = lax.fori_loop(
        0, blocks // group, index_scores, jnp.zeros((queries_count, fine), F32)
    )
    index_top = jnp.max(logits, axis=1, keepdims=True)
    index_total = jnp.sum(jnp.exp(logits - index_top), axis=1, keepdims=True)
    index_all[me] = to_row(index_top + jnp.log(index_total))
    lax.fori_loop(1, devices, index_start, 0)

    def sum_copy(half, sources, slots, target):
        return pltpu.make_async_remote_copy(
            src_ref=sum_send.at[half, sources],
            dst_ref=sum_recv.at[half, slots],
            send_sem=sum_send_sem.at[half],
            recv_sem=sum_recv_sem.at[half],
            device_id=(target, my_seq),
            device_id_type=MESH,
        )

    other_heads = pl.ds(0, heads_axis - 1)

    def combine(half, target):
        mine = expo[half, pl.ds(pl.multiple_of(target * fine, fine), fine), :]
        both = lax.dot_general(spread[half], mine, NT, preferred_element_type=F32)
        return both[0:half_queries] + both[half_queries : 2 * half_queries]

    own_parts = []
    for half in range(halves):
        stat_copy(half, other_seqs, my_seq).wait_recv()
        factor = jnp.exp2(base[half] - join_log2(stat_all[half]))
        upper = factor.astype(BF16).astype(F32)
        lower = factor - upper
        first = lax.broadcasted_iota(jnp.int32, (half_queries, 128), 0) * local_heads
        for j in range(half_rows // 128):
            lane = lax.broadcasted_iota(jnp.int32, (half_queries, 128), 1) + j * 128
            inside = jnp.logical_and(lane >= first, lane < first + local_heads)
            columns = slice(j * 128, (j + 1) * 128)
            spread[half, 0:half_queries, columns] = jnp.where(
                inside, upper[j : j + 1, :], 0.0
            ).astype(BF16)
            spread[half, half_queries : 2 * half_queries, columns] = jnp.where(
                inside, lower[j : j + 1, :], 0.0
            ).astype(BF16)
        for offset in range(1, heads_axis):
            target = lax.rem(my_head + offset, heads_axis)
            sum_send[half, target] = combine(half, target)
            sum_copy(half, target, my_head, target).start()
        own_parts.append(combine(half, my_head))

    for half in range(halves):
        sum_copy(half, other_heads, other_heads, my_head).wait_recv()
        for offset in range(1, heads_axis):
            source = lax.rem(my_head + offset, heads_axis)
            own_parts[half] = own_parts[half] + sum_recv[half, source]
    targets = jnp.concatenate(own_parts, axis=0) / heads
    index_copy(other_devices, me).wait_recv()
    index_log = to_column(join_log(index_all[...]), queries_count)
    shifted = logits - index_log
    positive = targets > 0
    own_loss = jnp.where(positive, targets * jnp.log(jnp.where(positive, targets, 1.0)), 0.0)
    own_loss = jnp.sum(own_loss - targets * shifted, axis=0, keepdims=True)
    own_loss = sum(own_loss[:, i * 128 : (i + 1) * 128] for i in range(fine // 128))
    grad = jnp.exp(shifted) - targets
    loss_all[me] = own_loss

    def loss_copy(slots, target):
        return pltpu.make_async_remote_copy(
            src_ref=loss_all.at[slots],
            dst_ref=loss_all.at[slots],
            send_sem=loss_send_sem.at[0],
            recv_sem=loss_recv_sem.at[0],
            device_id=place(target),
            device_id_type=MESH,
        )

    chunk = own_term.shape[1]
    owners = block // chunk
    depth, peers = term_a.shape[0:2]
    inner = seq_axis // depth
    lanes = inner // 2
    my_depth = my_seq // inner
    my_inner = lax.rem(my_seq, inner)
    parity = lax.rem(my_seq, 2)
    pair = my_seq + 1 - 2 * parity
    my_peer = my_head * lanes + my_inner // 2

    def peer_at(offset):
        return lax.rem(my_peer + offset, peers)

    def depth_at(distance):
        return lax.rem(my_depth + distance, depth)

    def owner_of(layer, peer, side):
        return (peer // lanes) * seq_axis + layer * inner + 2 * lax.rem(peer, lanes) + side

    every_peer = pl.ds(0, peers)
    other_peers = pl.ds(0, peers - 1)
    other_layers = pl.ds(0, depth - 1)

    def pair_copy(layer, slots):
        return pltpu.make_async_remote_copy(
            src_ref=own_term.at[slots],
            dst_ref=pair_recv.at[slots],
            send_sem=pair_send_sem.at[0],
            recv_sem=pair_recv_sem.at[layer],
            device_id=(my_head, pair),
            device_id_type=MESH,
        )

    def plane_copy(layer, sources, slots, target):
        return pltpu.make_async_remote_copy(
            src_ref=term_a.at[layer, sources],
            dst_ref=recv_a.at[layer, slots],
            send_sem=a_send_sem.at[layer],
            recv_sem=a_recv_sem.at[layer],
            device_id=(target // lanes, my_depth * inner + 2 * lax.rem(target, lanes) + parity),
            device_id_type=MESH,
        )

    def depth_copy(sources, slots, target):
        return pltpu.make_async_remote_copy(
            src_ref=term_b.at[sources],
            dst_ref=recv_b.at[slots],
            send_sem=b_send_sem.at[0],
            recv_sem=b_recv_sem.at[0],
            device_id=(my_head, target * inner + my_inner),
            device_id_type=MESH,
        )

    grads = jnp.concatenate([grad] * heads_in_block, axis=0)
    grad_upper = grads.astype(BF16).astype(F32)
    grad_lower = grads - grad_upper

    def back(chosen):
        upper_parts, lower_parts = [], []
        for b in chosen:
            part = act[b]
            on = part > 0
            dact[b] = jnp.where(on, grads * weights[b], 0.0).astype(BF16)
            upper_parts.append(jnp.where(on, grad_upper, 0.0).astype(BF16))
            lower_parts.append(jnp.where(on, grad_lower, 0.0).astype(BF16))
        both = jnp.concatenate(upper_parts + lower_parts, axis=0)
        result = jnp.dot(both, keys_ref[...], preferred_element_type=F32)
        result = result[0 : block * len(chosen)] + result[block * len(chosen) :]
        for i, b in enumerate(chosen):
            for j in range(owners):
                start = i * block + j * chunk
                own_term[b * owners + j] = result[start : start + chunk]

    def layer_at(step):
        up = step + jnp.where(step >= my_depth, 1, 0)
        down = depth - 1 - step
        down = down - jnp.where(down <= my_depth, 1, 0)
        return jnp.where(step >= depth - 1, my_depth, jnp.where(2 * my_depth >= depth, up, down))

    def pair_start(layer):
        for offset in range(peers):
            pair_copy(layer, owner_of(layer, peer_at(offset), 1 - parity)).start()

    def plane_start(layer):
        pair_copy(layer, every_peer).wait_recv()
        for offset in range(1, peers):
            peer = peer_at(offset)
            owner = owner_of(layer, peer, parity)
            term_a[layer, peer] = (own_term[owner] + pair_recv[owner]).astype(BF16)
            plane_copy(layer, peer, my_peer, peer).start()

    def layer_back(layer, side):
        if owners == 1:
            back([owner_of(layer, peer_at(offset), side) for offset in range(peers)])

    if owners > 1:

        def every_block(b, carry):
            back([b])
            return carry

        lax.fori_loop(0, blocks, every_block, 0)

    layer_back(layer_at(0), 1 - parity)
    pair_start(layer_at(0))

    def loss_start(offset, carry):
        loss_copy(me, lax.rem(me + offset, devices)).start()
        return carry


    def mixed(step, carry):
        ahead = layer_at(step + 1)
        layer_back(ahead, 1 - parity)
        pair_start(ahead)
        layer = layer_at(step)
        layer_back(layer, parity)
        plane_start(layer)
        return carry

    lax.fori_loop(0, depth - 1, mixed, 0)
    lax.fori_loop(1, devices, loss_start, 0)
    layer_back(my_depth, parity)
    plane_start(my_depth)

    key_out[...] = lax.dot_general(
        dact[...].reshape(blocks * block, fine),
        idx_q[...].reshape(blocks * block, -1),
        TN,
        preferred_element_type=F32,
    )

    for half in range(halves):
        stat_copy(half, other_seqs, my_seq).wait_send()
        sum_copy(half, other_heads, other_heads, my_head).wait_send()
    index_copy(other_devices, me).wait_send()

    pair_copy(0, pl.ds(0, depth * peers)).wait_send()

    def plane_total(layer):
        owner = owner_of(layer, my_peer, parity)
        plane_copy(layer, other_peers, other_peers, my_peer).wait_recv()
        total = own_term[owner] + pair_recv[owner]
        for offset in range(1, peers):
            total = total + recv_a[layer, peer_at(offset)].astype(F32)
        return total

    def depth_start(step, carry):
        layer = layer_at(step)
        term_b[layer] = plane_total(layer).astype(BF16)
        depth_copy(layer, my_depth, layer).start()
        return carry

    lax.fori_loop(0, depth - 1, depth_start, 0)
    total = plane_total(my_depth)
    if depth > 1:
        depth_copy(other_layers, other_layers, my_depth).wait_recv()
    for distance in range(1, depth):
        total = total + recv_b[depth_at(distance)].astype(F32)
    own_block = me // owners
    inside_block = me - own_block * owners
    own_weights = weights[own_block]
    own_queries = idx_q[own_block].astype(F32)
    if owners == 1:
        query_out[...] = total * own_weights
        prod_out[...] = total * own_queries
    else:
        for j in range(owners):

            @pl.when(inside_block == j)
            def _():
                query_out[...] = total * own_weights[j * chunk : (j + 1) * chunk]
                prod_out[...] = total * own_queries[j * chunk : (j + 1) * chunk]

    loss_copy(other_devices, me).wait_recv()
    loss_out[...] = jnp.sum(loss_all[...], axis=0)
    loss_copy(other_devices, me).wait_send()

    def plane_sent(layer, carry):
        plane_copy(layer, other_peers, other_peers, my_peer).wait_send()
        return carry

    lax.fori_loop(0, depth, plane_sent, 0)
    if depth > 1:
        depth_copy(other_layers, other_layers, my_depth).wait_send()


def closing(queries_count, loss_in, query_in, prod_in, key_in, loss_out, query_out, weight_out, key_out, sems):
    copies = [
        pltpu.make_async_copy(key_in, key_out, sems.at[0]),
        pltpu.make_async_copy(query_in, query_out, sems.at[1]),
    ]
    for copy in copies:
        copy.start()
    loss_out[...] = jnp.sum(loss_in[...], axis=1, keepdims=True) / queries_count
    ones = jnp.ones((8, prod_in.shape[1]), F32)
    sums = lax.dot_general(
        ones, prod_in[...], NT, precision=lax.Precision.HIGHEST, preferred_element_type=F32
    )
    weight_out[...] = sums[0:1]
    for copy in copies:
        copy.wait()


def shards(heads_axis, seq_axis, latent_q, latent_keys, idx_q, idx_keys, idx_weight):
    queries_count, local_heads, width = latent_q.shape
    index_heads, size = idx_q.shape[1:]
    rows = queries_count * local_heads
    keys = latent_keys.shape[0]
    fine = idx_keys.shape[1]
    devices = heads_axis * seq_axis
    all_rows = queries_count * index_heads
    chunk = all_rows // devices
    block = max(chunk, queries_count)
    blocks = all_rows // block
    halves = 2
    half_rows = rows // halves
    half_queries = queries_count // halves
    tile = min(256, half_rows)
    inner = math.gcd(seq_axis, 4)
    depth = seq_axis // inner
    peers = heads_axis * inner // 2
    queries = idx_q.reshape(all_rows, size)
    vmem = pl.BlockSpec(memory_space=pltpu.VMEM)
    dma = pltpu.SemaphoreType.DMA
    loss, query_grad, prod, key_grad = pl.pallas_call(
        functools.partial(
            kernel, heads_axis, seq_axis, local_heads * heads_axis, queries_count
        ),
        out_shape=(
            pltpu.VMEM((1, 128), F32),
            pltpu.VMEM((chunk, size), F32),
            pltpu.VMEM((chunk, size), F32),
            pltpu.VMEM((fine, size), F32),
        ),
        in_specs=[pl.BlockSpec(memory_space=pltpu.HBM)] * 5,
        out_specs=(vmem,) * 4,
        scratch_shapes=[
            pltpu.VMEM((rows, width), BF16),
            pltpu.VMEM((width, keys), BF16),
            pltpu.VMEM((all_rows, size), BF16),
            pltpu.VMEM((fine, size), BF16),
            pltpu.VMEM((queries_count, index_heads), BF16),
            dma((halves + 4,)),
            pltpu.VMEM((keys, width), BF16),
            pltpu.VMEM((keys, tile), F32),
            pltpu.VMEM((keys, tile), F32),
            pltpu.VMEM((1, tile), F32),
            pltpu.VMEM((1, tile), F32),
            pltpu.VMEM((blocks, block, size), BF16),
            pltpu.VMEM((all_rows, size), F32),
            pltpu.VMEM((blocks, block, 1), F32),
            pltpu.VMEM((devices, chunk, size), F32),
            pltpu.VMEM((devices, chunk, size), F32),
            pltpu.VMEM((devices, 1, 128), F32),
            pltpu.VMEM((halves, keys, half_rows), BF16),
            pltpu.VMEM((halves, half_rows // 128, 128), F32),
            pltpu.VMEM((halves, 2 * half_queries, half_rows), BF16),
            pltpu.VMEM((halves, seq_axis, half_rows // 128, 128), F32),
            pltpu.VMEM((halves, heads_axis, half_queries, fine), F32),
            pltpu.VMEM((halves, heads_axis, half_queries, fine), F32),
            pltpu.VMEM((blocks, block, fine), F32),
            pltpu.VMEM((blocks, block, fine), BF16),
            pltpu.VMEM((depth, peers, chunk, size), BF16),
            pltpu.VMEM((depth, peers, chunk, size), BF16),
            pltpu.VMEM((depth, chunk, size), BF16),
            pltpu.VMEM((depth, chunk, size), BF16),
            pltpu.VMEM((devices, 1, 128), F32),
            dma((halves,)),
            dma((halves,)),
            dma((halves,)),
            dma((halves,)),
            dma((depth,)),
            dma((depth,)),
            dma((1,)),
            dma((1,)),
            dma((1,)),
            dma((1,)),
            dma((1,)),
            dma((depth,)),
            dma((1,)),
            dma((1,)),
        ],
        compiler_params=pltpu.CompilerParams(
            collective_id=0, has_side_effects=True, vmem_limit_bytes=56 * 1024 * 1024
        ),
    )(latent_q.reshape(rows, width), latent_keys.T, queries, idx_keys[0], idx_weight)
    held = [
        pltpu.with_memory_space_constraint(x, pltpu.VMEM)
        for x in (loss, query_grad, prod, key_grad)
    ]
    hbm = pl.BlockSpec(memory_space=pltpu.HBM)
    loss, query_grad, weight_grad, key_grad = pl.pallas_call(
        functools.partial(closing, queries_count),
        out_shape=(
            jax.ShapeDtypeStruct((1, 1), F32),
            jax.ShapeDtypeStruct((chunk, size), F32),
            jax.ShapeDtypeStruct((1, chunk), F32),
            jax.ShapeDtypeStruct((fine, size), F32),
        ),
        in_specs=[vmem] * 4,
        out_specs=(vmem, hbm, vmem, hbm),
        scratch_shapes=[dma((2,))],
    )(*held)
    return (loss.reshape(()), query_grad, weight_grad.reshape(-1), key_grad[None])


def solution(mesh):
    in_specs = (P(None, "head", None), P("seq", None), P(), P("seq", "head", None), P())
    out_specs = (P(), P(("head", "seq"), None), P(("head", "seq")), P("seq", "head", None))
    body = functools.partial(shards, mesh.shape["head"], mesh.shape["seq"])
    return jax.shard_map(body, mesh=mesh, in_specs=in_specs, out_specs=out_specs, check_vma=False)
```
